256 devices in a mesh: out: 16 (over z, x_lo), inp: 16 (over y, x_hi, core).
Axes of the slice: x: 4 (x_hi: 2, x_lo: 2; x = x_hi * 2 + x_lo), y: 4, z: 8, core: 2. Of those that a mesh axis runs over, the one named last changes fastest.
Arguments:
- tensor: bfloat16 [1024, 1024, 1024], P('out', 'inp'), may hold values from -0.005859375 to 0.005859375
- state: bfloat16 [1536, 1024], P('out'), may hold values from -6 to 6
Outputs:
- collision: bfloat16 [1536, 1024], P('inp', 'out')
The draws below stay inside these ranges and needn't reach their ends.
All inputs are finite; a program needn't handle non-finite values.
Results may differ from the reference program's by a relative error of at most 0.001.
Values may be sent and summed in bfloat16 or wider, within the bound.
No kernel may reach another device: no remote copies, remote signals or barrier semaphores. Data moves between devices by JAX's collectives and lax.ppermute only.
A program may use at most 64 MiB of HBM per device.

```python
import jax
import jax.numpy as jnp
from jax import lax

K = 1024
CELLS = 1536


def shard_levels(key, shape, split, least, high):
    loudness, own = 1.0, jax.random.fold_in(key, 6)
    for dim, shards_of in split:
        steps = jnp.exp(jax.random.uniform(jax.random.fold_in(own, dim), (shards_of,), jnp.float32, least / len(split), high / len(split)))
        loudness = loudness * jnp.repeat(steps, shape[dim] // shards_of).reshape([-1 if axis == dim else 1 for axis in range(len(shape))])
    return loudness


def centred(own_key, extent, scale, most, shards=(), kind=jnp.bfloat16):
    drawn = jax.random.normal(own_key, extent, jnp.float32) * scale
    if len(shards) > 0:
        drawn = shard_levels(own_key, extent, shards, -0.22, 0.18) * drawn
    return jnp.clip(drawn, min=-most, max=most).astype(kind)


def setup_inputs(seed: int = 0) -> dict:
    key_list = jax.random.split(jax.random.key(seed), 3)
    return {
        "tensor": centred(key_list[0], (K, K, K), (K * K) ** -0.5, 0.005859375, ((0, 16), (1, 16))),
        "state": centred(key_list[1], (CELLS, K), 1.0, 6.0, ((0, 16),)),
    }


def reference(tensor, state):
    blocks = tensor.reshape(K // 16, 16, K, K)
    state_wide = state.astype(jnp.float32)

    def one_block(slab):
        flat = slab.reshape(16 * K, K)
        inner = lax.dot_general(state, flat, (((1,), (1,)), ((), ())), preferred_element_type=jnp.float32)
        inner = inner.reshape(state.shape[0], 16, K)
        return jnp.sum(inner * state_wide[:, None, :], axis=2)

    parts = lax.map(one_block, blocks)
    result = jnp.transpose(parts, (1, 0, 2)).reshape(state.shape[0], K)
    return result.astype(jnp.bfloat16)
```

```python
import functools

import jax
import jax.numpy as jnp
from jax import lax
from jax.experimental import pallas as pl
from jax.experimental.pallas import tpu as pltpu
from jax.sharding import PartitionSpec as P

NZ, NX, NY, NC = 8, 4, 4, 2
AXES = ("out", "inp")
BLOCK = 96
HALF = BLOCK // 2
K_OUT = 64
K_INP = 64
K_STEP = 32
TILE = 256
NEAR = (0, 1, 2, -1, -2)
FAR = (3, -3, 4)
VMEM = pl.BlockSpec(memory_space=pltpu.VMEM)
SMEM = pl.BlockSpec(memory_space=pltpu.SMEM)
HBM = pl.BlockSpec(memory_space=pltpu.HBM)

SMALL = pltpu.CompilerParams(vmem_limit_bytes=4 << 20)


def device(x, y, z, core):
    out = (z % NZ) * 2 + (x % NX) % 2
    inp = (y % NY) * 4 + ((x % NX) // 2) * 2 + core % NC
    return out * 16 + inp


def hop(way):
    pairs = []
    for z in range(NZ):
        for y in range(NY):
            for x in range(NX):
                for c in range(NC):
                    dx, dy, dz, dc = way(c)
                    pairs.append((device(x, y, z, c), device(x + dx, y + dy, z + dz, c + dc)))
    return pairs


def sign(core):
    return 1 - 2 * core


def along_z(array, d):
    return lax.ppermute(array, AXES, hop(lambda c: (0, 0, d * sign(c), 0)))


def along_x(array):
    return lax.ppermute(array, AXES, hop(lambda c: (sign(c), 0, 0, 0)))


def swap(array):
    return lax.ppermute(array, AXES, hop(lambda c: (0, 0, 0, 1)))


def rows(*arrays):
    return jnp.concatenate(arrays, axis=0)


def pack(block):
    last = block[48:64]
    side = jnp.concatenate([last[:, 0:32], last[:, 32:64], last[:, 64:96]], axis=0)
    return jnp.concatenate([block[0:48], side], axis=1)


def unpack(packed):
    side = packed[:, 96:128]
    last = jnp.concatenate([side[0:16], side[16:32], side[32:48]], axis=1)
    return jnp.concatenate([packed[:, 0:96], last], axis=0)


def place_group(cells, start, shards, mine, theirs, core):
    source = [0, 0]
    for n, d in enumerate(shards):
        at = start + n * BLOCK
        if d in (0, 4):
            for which, piece in enumerate((mine, theirs)):
                half = core if which == 0 else 1 - core
                first = 0 if d == 0 else BLOCK
                spot = pl.multiple_of(at + half * HALF, 16)
                cells[pl.ds(spot, HALF), :] = piece[first : first + HALF, :]
                if d == 0:
                    source[which] = HALF
        else:
            which, piece = (0, mine) if d > 0 else (1, theirs)
            first = source[which]
            cells[at : at + BLOCK, :] = piece[first : first + BLOCK, :]
            source[which] = first + BLOCK


def collide(groups, first_call, where, *refs):
    refs = list(refs)
    tensor_in = refs.pop(0)
    pieces = [(refs.pop(0), refs.pop(0)) for _ in groups]
    if first_call:
        give, keep, tensor, cells, weight, total, arrived = refs
        copies = [
            pltpu.make_async_copy(
                tensor_in.at[pl.ds(k, K_STEP)], tensor.at[pl.ds(k, K_STEP)], arrived.at[k // K_STEP]
            )
            for k in range(0, K_OUT, K_STEP)
        ]
        for copy in copies:
            copy.start()
    else:
        tensor = tensor_in
        _, _, give, keep, cells, weight, total = refs
        copies = None
    first, z, odd, core = where[0], where[1], where[2], where[3]
    start = 0
    for (shards, _), (mine, theirs) in zip(groups, pieces):
        place_group(cells, start, shards, mine, theirs, core)
        start += BLOCK * len(shards)
    base = pl.multiple_of((first // 128) * 128, 128)
    weight[...] = cells[:, pl.ds(base, 128)].astype(jnp.float32).T
    off = pl.multiple_of(lax.rem(first, 128), K_INP)
    size = cells.shape[0]

    def step(k):
        left = tensor[pl.ds(k, K_STEP)].reshape(K_STEP * K_INP, tensor.shape[2])
        for c in range(0, size, TILE):
            w = min(TILE, size - c)
            inner = lax.dot_general(
                left,
                cells[c : c + w, :],
                (((1,), (1,)), ((), ())),
                preferred_element_type=jnp.float32,
            )
            chosen = weight[pl.ds(off, K_INP), c : c + w]
            total[pl.ds(k, K_STEP), c : c + w] = jnp.sum(
                inner.reshape(K_STEP, K_INP, w) * chosen[None], axis=1
            )

    if copies is None:

        def body(s, carry):
            step(pl.multiple_of(s * K_STEP, K_STEP))
            return carry

        lax.fori_loop(0, K_OUT // K_STEP, body, 0)
    else:
        for n, copy in enumerate(copies):
            copy.wait()
            step(n * K_STEP)

    at = 0
    for shards, own in groups:
        kept = (odd == core) if own else (odd != core)
        blocks = []
        for d in shards:
            owner = lax.rem(z - d * (1 - 2 * core) + NZ, NZ)
            blocks.append((owner, pack(total[:, at : at + BLOCK])))
            at += BLOCK

        @pl.when(kept)
        def _():
            for owner, block in blocks:
                keep[owner] = block

        @pl.when(jnp.logical_not(kept))
        def _():
            for owner, block in blocks:
                give[owner] = block


def partial_sums(groups, where, tensor, pieces, before):
    size = BLOCK * sum(len(shards) for shards, _ in groups)
    first_call = before is None
    args = [where, tensor] + [piece for pair in pieces for piece in pair]
    in_specs = [SMEM, HBM if first_call else VMEM] + [VMEM] * (len(args) - 2)
    part = jax.ShapeDtypeStruct((NZ, 48, 128), jnp.float32)
    out_shape, aliases = [part, part], {}
    scratch = [
        pltpu.VMEM((size, 1024), jnp.bfloat16),
        pltpu.VMEM((128, size), jnp.float32),
        pltpu.VMEM((K_OUT, size), jnp.float32),
    ]
    if first_call:
        out_shape.append(jax.ShapeDtypeStruct(tensor.shape, tensor.dtype))
        scratch.append(pltpu.SemaphoreType.DMA((K_OUT // K_STEP,)))
    else:
        aliases = {len(args): 0, len(args) + 1: 1}
        args += before
        in_specs += [VMEM, VMEM]
    return pl.pallas_call(
        functools.partial(collide, groups, first_call),
        in_specs=in_specs,
        out_specs=[VMEM] * len(out_shape),
        out_shape=out_shape,
        input_output_aliases=aliases,
        scratch_shapes=scratch,
        compiler_params=pltpu.CompilerParams(vmem_limit_bytes=(42 if first_call else 24) << 20),
        cost_estimate=pl.CostEstimate(
            flops=2 * K_OUT * K_INP * 1024 * size,
            bytes_accessed=1 << 20,
            transcendentals=0,
        ),
    )(*args)


def add_pair(mine, theirs, out):
    out[...] = mine[...] + theirs[...]


def add_up(shares, out):
    out[...] = unpack(jnp.sum(shares[...], axis=0)).astype(jnp.bfloat16)


def local(tensor, state):
    out_at, inp_at = lax.axis_index("out"), lax.axis_index("inp")
    z, odd, core = out_at // 2, out_at % 2, inp_at % 2
    where = jnp.stack([inp_at * K_INP, z, odd, core]).astype(jnp.int32)

    def half(array):
        return lax.dynamic_slice_in_dim(array, core * HALF, HALF, 0)

    one = along_z(state, 1)
    two = along_z(state, 2)
    near = rows(half(state), one, two)
    three = along_z(two, 1)
    four = along_z(half(two), 2)
    near_x = along_x(near)
    near_swap = swap(near)
    give, keep, held = partial_sums(
        ((NEAR, True),), where, tensor, [(near, near_swap)], None
    )

    three, four, give = lax.optimization_barrier((three, four, give))
    far = rows(three, four)
    far_x = along_x(far)
    far_swap = swap(far)
    near_x_swap = swap(near_x)
    give, keep = partial_sums(
        ((FAR, True), (NEAR, False)),
        where,
        held,
        [(far, far_swap), (near_x, near_x_swap)],
        [give, keep],
    )

    far_x, give = lax.optimization_barrier((far_x, give))
    far_x_swap = swap(far_x)
    give, keep = partial_sums(
        ((FAR, False),), where, held, [(far_x, far_x_swap)], [give, keep]
    )

    got = swap(give)
    pair = pl.pallas_call(
        add_pair,
        in_specs=[VMEM, VMEM],
        out_specs=VMEM,
        out_shape=jax.ShapeDtypeStruct(keep.shape, keep.dtype),
        compiler_params=SMALL,
    )(keep, got)
    groups = [[c + NC * i for i in range(NZ)] for c in range(NC)]
    shares = lax.all_to_all(pair, "inp", 0, 0, tiled=True, axis_index_groups=groups)
    done = pl.pallas_call(
        add_up,
        in_specs=[VMEM],
        out_specs=VMEM,
        out_shape=jax.ShapeDtypeStruct((K_OUT, BLOCK), jnp.bfloat16),
        compiler_params=SMALL,
    )(shares)
    return done.T


def solution(mesh):
    placed = (P("out", "inp", None), P("out", None))
    return jax.shard_map(
        local, mesh=mesh, in_specs=placed, out_specs=P("inp", "out"), check_vma=False
    )
```

```python
import functools

import jax
import jax.numpy as jnp
from jax import lax
from jax.experimental import pallas as pl
from jax.experimental.pallas import tpu as pltpu
from jax.sharding import PartitionSpec as P

NZ, NX, NY, NC = 8, 4, 4, 2
AXES = ("out", "inp")
BLOCK = 96
HALF = BLOCK // 2
K_OUT = 64
K_INP = 64
K_STEP = 32
TILE = 256
VMEM = pl.BlockSpec(memory_space=pltpu.VMEM)
SMEM = pl.BlockSpec(memory_space=pltpu.SMEM)
HBM = pl.BlockSpec(memory_space=pltpu.HBM)

SMALL = pltpu.CompilerParams(vmem_limit_bytes=4 << 20)


def device(x, y, z, core):
    out = (z % NZ) * 2 + (x % NX) % 2
    inp = (y % NY) * 4 + ((x % NX) // 2) * 2 + core % NC
    return out * 16 + inp


def hop(way):
    pairs = []
    for z in range(NZ):
        for y in range(NY):
            for x in range(NX):
                for c in range(NC):
                    dx, dy, dz, dc = way(c)
                    pairs.append((device(x, y, z, c), device(x + dx, y + dy, z + dz, c + dc)))
    return pairs


def sign(core):
    return 1 - 2 * core


def along_z(array, d):
    return lax.ppermute(array, AXES, hop(lambda c: (0, 0, d * sign(c), 0)))


def along_x(array):
    return lax.ppermute(array, AXES, hop(lambda c: (sign(c), 0, 0, 0)))


def swap(array):
    return lax.ppermute(array, AXES, hop(lambda c: (0, 0, 0, 1)))


def rows(*arrays):
    return jnp.concatenate(arrays, axis=0)


def pack(block):
    last = block[48:64]
    side = jnp.concatenate([last[:, 0:32], last[:, 32:64], last[:, 64:96]], axis=0)
    return jnp.concatenate([block[0:48], side], axis=1)


def unpack(packed):
    side = packed[:, 96:128]
    last = jnp.concatenate([side[0:16], side[16:32], side[32:48]], axis=1)
    return jnp.concatenate([packed[:, 0:96], last], axis=0)


def collide(plan, first_call, n_pieces, where, *refs):
    refs = list(refs)
    tensor_in = refs.pop(0)
    pieces, refs = refs[:n_pieces], refs[n_pieces:]
    if first_call:
        give, keep, tensor, cells, weight, total, arrived = refs
        copies = [
            pltpu.make_async_copy(
                tensor_in.at[pl.ds(k, K_STEP)], tensor.at[pl.ds(k, K_STEP)], arrived.at[k // K_STEP]
            )
            for k in range(0, K_OUT, K_STEP)
        ]
        for copy in copies:
            copy.start()
    else:
        tensor = tensor_in
        _, _, give, keep, cells, weight, total = refs
        copies = None
    first, z, odd, core = where[0], where[1], where[2], where[3]
    for n, (_, _, parts) in enumerate(plan):
        for piece, source, count, half in parts:
            at = n * BLOCK
            if half is not None:
                at = pl.multiple_of(at + (core if half == 0 else 1 - core) * HALF, 16)
            cells[pl.ds(at, count), :] = pieces[piece][source : source + count, :]
    base = pl.multiple_of((first // 128) * 128, 128)
    weight[...] = cells[:, pl.ds(base, 128)].astype(jnp.float32).T
    off = pl.multiple_of(lax.rem(first, 128), K_INP)
    size = cells.shape[0]

    for k in range(0, K_OUT, K_STEP):
        if copies is not None:
            copies[k // K_STEP].wait()
        left = tensor[pl.ds(k, K_STEP)].reshape(K_STEP * K_INP, tensor.shape[2])
        for c in range(0, size, TILE):
            w = min(TILE, size - c)
            inner = lax.dot_general(
                left,
                cells[c : c + w, :],
                (((1,), (1,)), ((), ())),
                preferred_element_type=jnp.float32,
            )
            chosen = weight[pl.ds(off, K_INP), c : c + w]
            total[pl.ds(k, K_STEP), c : c + w] = jnp.sum(
                inner.reshape(K_STEP, K_INP, w) * chosen[None], axis=1
            )

    for n, (d, own, _) in enumerate(plan):
        kept = (odd == core) if own else (odd != core)
        owner = lax.rem(z - d * (1 - 2 * core) + NZ, NZ)
        block = pack(total[:, n * BLOCK : (n + 1) * BLOCK])

        @pl.when(kept)
        def _(block=block, owner=owner):
            keep[owner] = block

        @pl.when(jnp.logical_not(kept))
        def _(block=block, owner=owner):
            give[owner] = block


def partial_sums(plan, where, tensor, pieces, before):
    size = BLOCK * len(plan)
    first_call = before is None
    args = [where, tensor, *pieces]
    in_specs = [SMEM, HBM if first_call else VMEM] + [VMEM] * len(pieces)
    part = jax.ShapeDtypeStruct((NZ, 48, 128), jnp.float32)
    out_shape, aliases = [part, part], {}
    scratch = [
        pltpu.VMEM((size, 1024), jnp.bfloat16),
        pltpu.VMEM((128, size), jnp.float32),
        pltpu.VMEM((K_OUT, size), jnp.float32),
    ]
    if first_call:
        out_shape.append(jax.ShapeDtypeStruct(tensor.shape, tensor.dtype))
        scratch.append(pltpu.SemaphoreType.DMA((K_OUT // K_STEP,)))
    else:
        aliases = {len(args): 0, len(args) + 1: 1}
        args += before
        in_specs += [VMEM, VMEM]
    return pl.pallas_call(
        functools.partial(collide, plan, first_call, len(pieces)),
        in_specs=in_specs,
        out_specs=[VMEM] * len(out_shape),
        out_shape=out_shape,
        input_output_aliases=aliases,
        scratch_shapes=scratch,
        compiler_params=pltpu.CompilerParams(
            vmem_limit_bytes=(42 if first_call else 24) << 20
        ),
        cost_estimate=pl.CostEstimate(
            flops=2 * K_OUT * K_INP * 1024 * size,
            bytes_accessed=tensor.size * 4 if first_call else 1 << 20,
            transcendentals=0,
        ),
    )(*args)


def whole(piece, source=0):
    return ((piece, source, BLOCK, None),)


def halves(mine, theirs, source):
    return ((mine, source, HALF, 0), (theirs, source, HALF, 1))


def add_pair(mine, theirs, out):
    out[...] = mine[...] + theirs[...]


def add_up(shares, out):
    out[...] = unpack(jnp.sum(shares[...], axis=0)).astype(jnp.bfloat16)


def local(tensor, state):
    out_at, inp_at = lax.axis_index("out"), lax.axis_index("inp")
    z, odd, core = out_at // 2, out_at % 2, inp_at % 2
    where = jnp.stack([inp_at * K_INP, z, odd, core]).astype(jnp.int32)

    def half(array):
        return lax.dynamic_slice_in_dim(array, core * HALF, HALF, 0)

    one = along_z(state, 1)
    two = along_z(state, 2)
    give, keep, held = partial_sums(((0, True, whole(0)),), where, tensor, [state], None)

    three = along_z(two, 1)
    four = along_z(half(two), 2)
    near_x = along_x(rows(state, one, two))
    near_swap = swap(rows(one, two))
    plan = ((1, True, whole(0)), (2, True, whole(1)))
    give, keep = partial_sums(plan, where, held, [one, two], [give, keep])

    three, four, give = lax.optimization_barrier((three, four, give))
    far = rows(three, four)
    far_x = along_x(far)
    far_swap = swap(far)
    near_x_swap = swap(near_x[BLOCK:])
    plan = (
        (-1, True, whole(0)),
        (-2, True, whole(0, BLOCK)),
        (3, True, whole(1)),
        (-3, True, whole(2)),
        (4, True, halves(1, 2, BLOCK)),
        (0, False, whole(3)),
        (1, False, whole(3, BLOCK)),
        (2, False, whole(3, 2 * BLOCK)),
    )
    give, keep = partial_sums(
        plan, where, held, [near_swap, far, far_swap, near_x], [give, keep]
    )

    far_x, give = lax.optimization_barrier((far_x, give))
    far_x_swap = swap(far_x)
    plan = (
        (-1, False, whole(0)),
        (-2, False, whole(0, BLOCK)),
        (3, False, whole(1)),
        (-3, False, whole(2)),
        (4, False, halves(1, 2, BLOCK)),
    )
    give, keep = partial_sums(
        plan, where, held, [near_x_swap, far_x, far_x_swap], [give, keep]
    )

    got = swap(give)
    pair = pl.pallas_call(
        add_pair,
        in_specs=[VMEM, VMEM],
        out_specs=VMEM,
        out_shape=jax.ShapeDtypeStruct(keep.shape, keep.dtype),
        compiler_params=SMALL,
    )(keep, got)
    groups = [[c + NC * i for i in range(NZ)] for c in range(NC)]
    shares = lax.all_to_all(pair, "inp", 0, 0, tiled=True, axis_index_groups=groups)
    done = pl.pallas_call(
        add_up,
        in_specs=[VMEM],
        out_specs=VMEM,
        out_shape=jax.ShapeDtypeStruct((K_OUT, BLOCK), jnp.bfloat16),
        compiler_params=SMALL,
    )(shares)
    return done.T


def solution(mesh):
    placed = (P("out", "inp", None), P("out", None))
    return jax.shard_map(
        local, mesh=mesh, in_specs=placed, out_specs=P("inp", "out"), check_vma=False
    )
```

```python
import functools

import jax
import jax.numpy as jnp
from jax import lax
from jax.experimental import pallas as pl
from jax.experimental.pallas import tpu as pltpu
from jax.sharding import PartitionSpec as P

NZ, NX, NY, NC = 8, 4, 4, 2
AXES = ("out", "inp")
BLOCK = 96
HALF = BLOCK // 2
K_OUT = 64
K_INP = 64
K_STEP = 32
TILE = 256
VMEM = pl.BlockSpec(memory_space=pltpu.VMEM)
SMEM = pl.BlockSpec(memory_space=pltpu.SMEM)
HBM = pl.BlockSpec(memory_space=pltpu.HBM)

SMALL = pltpu.CompilerParams(vmem_limit_bytes=4 << 20)


def device(x, y, z, core):
    out = (z % NZ) * 2 + (x % NX) % 2
    inp = (y % NY) * 4 + ((x % NX) // 2) * 2 + core % NC
    return out * 16 + inp


def hop(way):
    pairs = []
    for z in range(NZ):
        for y in range(NY):
            for x in range(NX):
                for c in range(NC):
                    dx, dy, dz, dc = way(c)
                    pairs.append((device(x, y, z, c), device(x + dx, y + dy, z + dz, c + dc)))
    return pairs


def sign(core):
    return 1 - 2 * core


def along_z(array, d):
    return lax.ppermute(array, AXES, hop(lambda c: (0, 0, d * sign(c), 0)))


def along_x(array):
    return lax.ppermute(array, AXES, hop(lambda c: (sign(c), 0, 0, 0)))


def swap(array):
    return lax.ppermute(array, AXES, hop(lambda c: (0, 0, 0, 1)))


def rows(*arrays):
    return jnp.concatenate(arrays, axis=0)


def pack(block):
    last = block[48:64]
    side = jnp.concatenate([last[:, 0:32], last[:, 32:64], last[:, 64:96]], axis=0)
    return jnp.concatenate([block[0:48], side], axis=1)


def unpack(packed):
    side = packed[:, 96:128]
    last = jnp.concatenate([side[0:16], side[16:32], side[32:48]], axis=1)
    return jnp.concatenate([packed[:, 0:96], last], axis=0)


def collide(plan, first_call, n_pieces, where, *refs):
    refs = list(refs)
    tensor_in = refs.pop(0)
    pieces, refs = refs[:n_pieces], refs[n_pieces:]
    if first_call:
        give, keep, tensor, cells, weight, total, arrived = refs
        copies = [
            pltpu.make_async_copy(pieces[0], cells, arrived.at[0]),
            pltpu.make_async_copy(tensor_in, tensor, arrived.at[1]),
        ]
        for copy in copies:
            copy.start()
        for copy in copies:
            copy.wait()
    else:
        tensor = tensor_in
        _, _, give, keep, cells, weight, total = refs
    first, z, odd, core = where[0], where[1], where[2], where[3]
    for n, (_, _, parts) in enumerate(plan):
        for piece, source, count, half in parts:
            at = n * BLOCK
            if half is not None:
                at = pl.multiple_of(at + (core if half == 0 else 1 - core) * HALF, 16)
            cells[pl.ds(at, count), :] = pieces[piece][source : source + count, :]
    base = pl.multiple_of((first // 128) * 128, 128)
    weight[...] = cells[:, pl.ds(base, 128)].astype(jnp.float32).T
    off = pl.multiple_of(lax.rem(first, 128), K_INP)
    size = cells.shape[0]

    for k in range(0, K_OUT, K_STEP):
        left = tensor[pl.ds(k, K_STEP)].reshape(K_STEP * K_INP, tensor.shape[2])
        for c in range(0, size, TILE):
            w = min(TILE, size - c)
            inner = lax.dot_general(
                left,
                cells[c : c + w, :],
                (((1,), (1,)), ((), ())),
                preferred_element_type=jnp.float32,
            )
            chosen = weight[pl.ds(off, K_INP), c : c + w]
            total[pl.ds(k, K_STEP), c : c + w] = jnp.sum(
                inner.reshape(K_STEP, K_INP, w) * chosen[None], axis=1
            )

    for n, (d, own, _) in enumerate(plan):
        kept = (odd == core) if own else (odd != core)
        owner = lax.rem(z - d * (1 - 2 * core) + NZ, NZ)
        block = pack(total[:, n * BLOCK : (n + 1) * BLOCK])

        @pl.when(kept)
        def _(block=block, owner=owner):
            keep[owner] = block

        @pl.when(jnp.logical_not(kept))
        def _(block=block, owner=owner):
            give[owner] = block


def partial_sums(plan, where, tensor, pieces, before):
    size = BLOCK * len(plan)
    first_call = before is None
    args = [where, tensor, *pieces]
    in_specs = [SMEM] + [HBM if first_call else VMEM] * (1 + len(pieces))
    part = jax.ShapeDtypeStruct((NZ, 48, 128), jnp.float32)
    out_shape, aliases = [part, part], {}
    scratch = [
        pltpu.VMEM((size, 1024), jnp.bfloat16),
        pltpu.VMEM((128, size), jnp.float32),
        pltpu.VMEM((K_OUT, size), jnp.float32),
    ]
    if first_call:
        out_shape.append(jax.ShapeDtypeStruct(tensor.shape, tensor.dtype))
        scratch.append(pltpu.SemaphoreType.DMA((2,)))
    else:
        aliases = {len(args): 0, len(args) + 1: 1}
        args += before
        in_specs += [VMEM, VMEM]
    return pl.pallas_call(
        functools.partial(collide, plan, first_call, len(pieces)),
        in_specs=in_specs,
        out_specs=[VMEM] * len(out_shape),
        out_shape=out_shape,
        input_output_aliases=aliases,
        scratch_shapes=scratch,
        compiler_params=pltpu.CompilerParams(vmem_limit_bytes=16 << 20),
        cost_estimate=pl.CostEstimate(
            flops=2 * K_OUT * K_INP * 1024 * size,
            bytes_accessed=tensor.size * 4 if first_call else 1 << 20,
            transcendentals=0,
        ),
    )(*args)


def whole(piece, source=0):
    return ((piece, source, BLOCK, None),)


def halves(mine, theirs, source):
    return ((mine, source, HALF, 0), (theirs, source, HALF, 1))


def add_pair(mine, theirs, out):
    out[...] = mine[...] + theirs[...]


def add_up(shares, out):
    out[...] = unpack(jnp.sum(shares[...], axis=0)).astype(jnp.bfloat16)


def local(tensor, state):
    out_at, inp_at = lax.axis_index("out"), lax.axis_index("inp")
    z, odd, core = out_at // 2, out_at % 2, inp_at % 2
    start = core * HALF
    where = jnp.stack([inp_at * K_INP, z, odd, core, start]).astype(jnp.int32)

    def half(array):
        return lax.dynamic_slice(
            array, (start, 0), (HALF, array.shape[1]), allow_negative_indices=False
        )

    two = along_z(state, 2)
    one = along_z(state, 1)
    same_x = along_x(state)
    there = [pltpu.with_memory_space_constraint(a, pltpu.HBM) for a in (tensor, state)]
    give, keep, held = partial_sums(((0, True, ()),), where, there[0], there[1:], None)

    one, two, same_x, give = lax.optimization_barrier((one, two, same_x, give))
    near = rows(one, two)
    near_swap = swap(near)
    both = rows(one, half(two))
    near, both = lax.optimization_barrier((near, both))
    far = along_z(both, 2)
    near_x = along_x(near)
    plan = (
        (1, True, whole(0)),
        (2, True, whole(0, BLOCK)),
        (-1, True, whole(1)),
        (-2, True, whole(1, BLOCK)),
        (0, False, whole(2)),
    )
    give, keep = partial_sums(plan, where, held, [near, near_swap, same_x], [give, keep])

    far, give = lax.optimization_barrier((far, give))
    far_x = along_x(far)
    far_swap = swap(far)
    near_x_swap = swap(near_x)
    plan = (
        (3, True, whole(0)),
        (-3, True, whole(1)),
        (4, True, halves(0, 1, BLOCK)),
        (1, False, whole(2)),
        (2, False, whole(2, BLOCK)),
    )
    give, keep = partial_sums(plan, where, held, [far, far_swap, near_x], [give, keep])

    far_x, give = lax.optimization_barrier((far_x, give))
    far_x_swap = swap(far_x)
    plan = (
        (-1, False, whole(0)),
        (-2, False, whole(0, BLOCK)),
        (3, False, whole(1)),
        (-3, False, whole(2)),
        (4, False, halves(1, 2, BLOCK)),
    )
    give, keep = partial_sums(
        plan, where, held, [near_x_swap, far_x, far_x_swap], [give, keep]
    )

    got = swap(give)
    pair = pl.pallas_call(
        add_pair,
        in_specs=[VMEM, VMEM],
        out_specs=VMEM,
        out_shape=jax.ShapeDtypeStruct(keep.shape, keep.dtype),
        compiler_params=SMALL,
    )(keep, got)
    groups = [[c + NC * i for i in range(NZ)] for c in range(NC)]
    shares = lax.all_to_all(pair, "inp", 0, 0, tiled=True, axis_index_groups=groups)
    done = pl.pallas_call(
        add_up,
        in_specs=[VMEM],
        out_specs=VMEM,
        out_shape=jax.ShapeDtypeStruct((K_OUT, BLOCK), jnp.bfloat16),
        compiler_params=SMALL,
    )(shares)
    return done.T


def solution(mesh):
    placed = (P("out", "inp", None), P("out", None))
    return jax.shard_map(
        local, mesh=mesh, in_specs=placed, out_specs=P("inp", "out"), check_vma=False
    )
```

```python
import functools
from typing import NamedTuple

import jax
import jax.numpy as jnp
from jax import lax
from jax.experimental import pallas as pl
from jax.experimental.pallas import tpu as pltpu
from jax.sharding import PartitionSpec as P

NZ, NX, NY, NC = 8, 4, 4, 2
AXES = ("out", "inp")
BLOCK = 96
HALF = BLOCK // 2
K_OUT = 64
K_INP = 64
K_STEP = 32
TILE = 256
VMEM = pl.BlockSpec(memory_space=pltpu.VMEM)
SMEM = pl.BlockSpec(memory_space=pltpu.SMEM)
HBM = pl.BlockSpec(memory_space=pltpu.HBM)

SMALL = pltpu.CompilerParams(vmem_limit_bytes=4 << 20)


def device(x, y, z, core):
    out = (z % NZ) * 2 + (x % NX) % 2
    inp = (y % NY) * 4 + ((x % NX) // 2) * 2 + core % NC
    return out * 16 + inp


def hop(way):
    pairs = []
    for z in range(NZ):
        for y in range(NY):
            for x in range(NX):
                for c in range(NC):
                    dx, dy, dz, dc = way(c)
                    pairs.append((device(x, y, z, c), device(x + dx, y + dy, z + dz, c + dc)))
    return pairs


def sign(core):
    return 1 - 2 * core


def along_z(array, d):
    return lax.ppermute(array, AXES, hop(lambda c: (0, 0, d * sign(c), 0)))


def along_x(array):
    return lax.ppermute(array, AXES, hop(lambda c: (sign(c), 0, 0, 0)))


def swap(array):
    return lax.ppermute(array, AXES, hop(lambda c: (0, 0, 0, 1)))


def rows(*arrays):
    return jnp.concatenate(arrays, axis=0)


def pack(block):
    last = block[48:64]
    side = jnp.concatenate([last[:, 0:32], last[:, 32:64], last[:, 64:96]], axis=0)
    return jnp.concatenate([block[0:48], side], axis=1)


def unpack(packed):
    side = packed[:, 96:128]
    last = jnp.concatenate([side[0:16], side[16:32], side[32:48]], axis=1)
    return jnp.concatenate([packed[:, 0:96], last], axis=0)


def collide(call, where, *refs):
    refs = list(refs)
    tensor_in = refs.pop(0)
    n = len({part[0] for part in call.parts})
    pieces, refs = refs[:n], refs[n:]
    if call.kind == "first":
        give, keep, tensor, cells, weight, total, arrived = refs
        copies = [
            pltpu.make_async_copy(pieces[0], cells, arrived.at[0]),
            pltpu.make_async_copy(tensor_in, tensor, arrived.at[1]),
        ]
        for copy in copies:
            copy.start()
        for copy in copies:
            copy.wait()
    else:
        tensor = tensor_in
        if call.kind == "open":
            _, _, give, keep, total, cells, weight = refs
        elif call.kind == "close":
            _, _, _, give, keep, total, cells, weight = refs
        else:
            _, _, give, keep, cells, weight, total = refs
        core = where[3]
        for piece, source, count, at, half in call.parts:
            at -= call.low
            if half is not None:
                at = pl.multiple_of(at + (core if half == 0 else 1 - core) * HALF, 16)
            cells[pl.ds(at, count), :] = pieces[piece][source : source + count, :]
    first, z, odd, core = where[0], where[1], where[2], where[3]
    base = pl.multiple_of((first // 128) * 128, 128)
    weight[...] = cells[:, pl.ds(base, 128)].astype(jnp.float32).T
    off = pl.multiple_of(lax.rem(first, 128), K_INP)
    size = cells.shape[0]

    for k in range(0, K_OUT, K_STEP):
        left = tensor[pl.ds(k, K_STEP)].reshape(K_STEP * K_INP, tensor.shape[2])
        for c in range(0, size, TILE):
            w = min(TILE, size - c)
            inner = lax.dot_general(
                left,
                cells[c : c + w, :],
                (((1,), (1,)), ((), ())),
                preferred_element_type=jnp.float32,
            )
            chosen = weight[pl.ds(off, K_INP), c : c + w]
            total[pl.ds(k, K_STEP), call.low + c : call.low + c + w] = jnp.sum(
                inner.reshape(K_STEP, K_INP, w) * chosen[None], axis=1
            )

    for at, d, own in call.blocks:
        kept = (odd == core) if own else (odd != core)
        owner = lax.rem(z - d * (1 - 2 * core) + NZ, NZ)
        block = pack(total[:, at : at + BLOCK])

        @pl.when(kept)
        def _(block=block, owner=owner):
            keep[owner] = block

        @pl.when(jnp.logical_not(kept))
        def _(block=block, owner=owner):
            give[owner] = block


class Call(NamedTuple):
    kind: str
    low: int
    high: int
    parts: tuple
    blocks: tuple


def partial_sums(call, where, tensor, pieces, before):
    size = call.high - call.low
    first_call = call.kind == "first"
    args = [where, tensor, *pieces]
    in_specs = [SMEM] + [HBM if first_call else VMEM] * (1 + len(pieces))
    part = jax.ShapeDtypeStruct((NZ, 48, 128), jnp.float32)
    out_shape = [part, part]
    scratch = [
        pltpu.VMEM((size, 1024), jnp.bfloat16),
        pltpu.VMEM((128, size), jnp.float32),
    ]
    if call.kind in ("open", "close"):
        out_shape.append(jax.ShapeDtypeStruct((K_OUT, 2 * TILE), jnp.float32))
    else:
        scratch.append(pltpu.VMEM((K_OUT, size), jnp.float32))
    if first_call:
        out_shape.append(jax.ShapeDtypeStruct(tensor.shape, tensor.dtype))
        scratch.append(pltpu.SemaphoreType.DMA((2,)))
    aliases = {len(args) + n: n for n in range(len(before))}
    args += before
    in_specs += [VMEM] * len(before)
    return pl.pallas_call(
        functools.partial(collide, call),
        in_specs=in_specs,
        out_specs=[VMEM] * len(out_shape),
        out_shape=out_shape,
        input_output_aliases=aliases,
        scratch_shapes=scratch,
        compiler_params=pltpu.CompilerParams(vmem_limit_bytes=16 << 20),
        cost_estimate=pl.CostEstimate(
            flops=2 * K_OUT * K_INP * 1024 * size,
            bytes_accessed=tensor.size * 4 if first_call else 1 << 20,
            transcendentals=0,
        ),
    )(*args)


def far_calls(near_blocks):
    at = [n * BLOCK for n in range(5)]
    early = TILE - at[2]
    first = Call(
        "open",
        0,
        TILE,
        ((0, 0, 2 * BLOCK, 0, None), (1, 0, early, at[2], None)),
        tuple((at[n], d, own) for n, (d, own) in enumerate(near_blocks[:2])),
    )
    second = Call(
        "close",
        TILE,
        5 * BLOCK,
        (
            (0, early, BLOCK - early, TILE, None),
            (1, 0, BLOCK, at[3], None),
            (0, BLOCK, HALF, at[4], 0),
            (1, BLOCK, HALF, at[4], 1),
        ),
        tuple((at[2 + n], d, near_blocks[2]) for n, d in enumerate((3, -3, 4))),
    )
    return first, second


def add_pair(mine, theirs, out):
    out[...] = mine[...] + theirs[...]


def add_up(shares, out):
    out[...] = unpack(jnp.sum(shares[...], axis=0)).astype(jnp.bfloat16)


def local(tensor, state):
    out_at, inp_at = lax.axis_index("out"), lax.axis_index("inp")
    z, odd, core = out_at // 2, out_at % 2, inp_at % 2
    start = core * HALF
    where = jnp.stack([inp_at * K_INP, z, odd, core, start]).astype(jnp.int32)

    def half(array):
        return lax.dynamic_slice(
            array, (start, 0), (HALF, array.shape[1]), allow_negative_indices=False
        )

    two = along_z(state, 2)
    one = along_z(state, 1)
    same_x = along_x(state)
    there = [pltpu.with_memory_space_constraint(a, pltpu.HBM) for a in (tensor, state)]
    give, keep, held = partial_sums(
        Call("first", 0, BLOCK, ((0, 0, BLOCK, 0, None),), ((0, 0, True),)), where, there[0], there[1:], []
    )

    one, two, same_x, give = lax.optimization_barrier((one, two, same_x, give))
    near = rows(one, two)
    near_swap = swap(near)
    both = rows(one, half(two))
    near, both = lax.optimization_barrier((near, both))
    far = along_z(both, 2)
    near_x = along_x(near)
    call = Call(
        "plain",
        0,
        5 * BLOCK,
        (
            (0, 0, 2 * BLOCK, 0, None),
            (1, 0, 2 * BLOCK, 2 * BLOCK, None),
            (2, 0, BLOCK, 4 * BLOCK, None),
        ),
        tuple(
            (n * BLOCK, d, own)
            for n, (d, own) in enumerate(
                ((1, True), (2, True), (-1, True), (-2, True), (0, False))
            )
        ),
    )
    give, keep = partial_sums(call, where, held, [near, near_swap, same_x], [give, keep])

    far, give = lax.optimization_barrier((far, give))
    far_x = along_x(far)
    far_swap = swap(far)
    near_x_swap = swap(near_x)
    first, second = far_calls(((1, False), (2, False), True))
    give, keep, sums = partial_sums(first, where, held, [near_x, far], [give, keep])
    give, keep, sums = partial_sums(
        second, where, held, [far, far_swap], [give, keep, sums]
    )

    far_x, give = lax.optimization_barrier((far_x, give))
    far_x_swap = swap(far_x)
    first, second = far_calls(((-1, False), (-2, False), False))
    give, keep, sums = partial_sums(
        first, where, held, [near_x_swap, far_x], [give, keep]
    )
    give, keep, sums = partial_sums(
        second, where, held, [far_x, far_x_swap], [give, keep, sums]
    )

    got = swap(give)
    pair = pl.pallas_call(
        add_pair,
        in_specs=[VMEM, VMEM],
        out_specs=VMEM,
        out_shape=jax.ShapeDtypeStruct(keep.shape, keep.dtype),
        compiler_params=SMALL,
    )(keep, got)
    groups = [[c + NC * i for i in range(NZ)] for c in range(NC)]
    shares = lax.all_to_all(pair, "inp", 0, 0, tiled=True, axis_index_groups=groups)
    done = pl.pallas_call(
        add_up,
        in_specs=[VMEM],
        out_specs=VMEM,
        out_shape=jax.ShapeDtypeStruct((K_OUT, BLOCK), jnp.bfloat16),
        compiler_params=SMALL,
    )(shares)
    return done.T


def solution(mesh):
    placed = (P("out", "inp", None), P("out", None))
    return jax.shard_map(
        local, mesh=mesh, in_specs=placed, out_specs=P("inp", "out"), check_vma=False
    )
```

```python
import functools

import jax
import jax.numpy as jnp
from jax import lax
from jax.experimental import pallas as pl
from jax.experimental.pallas import tpu as pltpu
from jax.sharding import PartitionSpec as P

NZ, NX, NY, NC = 8, 4, 4, 2
AXES = ("out", "inp")
BLOCK = 96
HALF = BLOCK // 2
K_OUT = 64
K_INP = 64
K_STEP = 32
TILE = 256
VMEM = pl.BlockSpec(memory_space=pltpu.VMEM)
SMEM = pl.BlockSpec(memory_space=pltpu.SMEM)
HBM = pl.BlockSpec(memory_space=pltpu.HBM)

SMALL = pltpu.CompilerParams(vmem_limit_bytes=4 << 20)


def device(x, y, z, core):
    out = (z % NZ) * 2 + (x % NX) % 2
    inp = (y % NY) * 4 + ((x % NX) // 2) * 2 + core % NC
    return out * 16 + inp


def hop(way):
    pairs = []
    for z in range(NZ):
        for y in range(NY):
            for x in range(NX):
                for c in range(NC):
                    dx, dy, dz, dc = way(c)
                    pairs.append((device(x, y, z, c), device(x + dx, y + dy, z + dz, c + dc)))
    return pairs


def sign(core):
    return 1 - 2 * core


def along_z(array, d):
    return lax.ppermute(array, AXES, hop(lambda c: (0, 0, d * sign(c), 0)))


def along_x(array):
    return lax.ppermute(array, AXES, hop(lambda c: (sign(c), 0, 0, 0)))


def swap(array):
    return lax.ppermute(array, AXES, hop(lambda c: (0, 0, 0, 1)))


def rows(*arrays):
    return jnp.concatenate(arrays, axis=0)


def pack(block):
    last = block[48:64]
    side = jnp.concatenate([last[:, 0:32], last[:, 32:64], last[:, 64:96]], axis=0)
    return jnp.concatenate([block[0:48], side], axis=1)


def unpack(packed):
    side = packed[:, 96:128]
    last = jnp.concatenate([side[0:16], side[16:32], side[32:48]], axis=1)
    return jnp.concatenate([packed[:, 0:96], last], axis=0)


def collide(plan, first_call, n_pieces, where, *refs):
    refs = list(refs)
    tensor_in = refs.pop(0)
    pieces, refs = refs[:n_pieces], refs[n_pieces:]
    if first_call:
        give, keep, tensor, cells, weight, total, arrived = refs
        copies = [
            pltpu.make_async_copy(pieces[0], cells, arrived.at[0]),
            pltpu.make_async_copy(tensor_in, tensor, arrived.at[1]),
        ]
        for copy in copies:
            copy.start()
        for copy in copies:
            copy.wait()
    else:
        tensor = tensor_in
        _, _, give, keep, cells, weight, total = refs
    first, z, odd, core = where[0], where[1], where[2], where[3]
    for n, (_, _, parts) in enumerate(plan):
        for piece, source, count, half in parts:
            at = n * BLOCK
            if half is not None:
                at = pl.multiple_of(at + (core if half == 0 else 1 - core) * HALF, 16)
            cells[pl.ds(at, count), :] = pieces[piece][source : source + count, :]
    base = pl.multiple_of((first // 128) * 128, 128)
    weight[...] = cells[:, pl.ds(base, 128)].astype(jnp.float32).T
    off = pl.multiple_of(lax.rem(first, 128), K_INP)
    size = cells.shape[0]

    for k in range(0, K_OUT, K_STEP):
        left = tensor[pl.ds(k, K_STEP)].reshape(K_STEP * K_INP, tensor.shape[2])
        for c in range(0, size, TILE):
            w = min(TILE, size - c)
            inner = lax.dot_general(
                left,
                cells[c : c + w, :],
                (((1,), (1,)), ((), ())),
                preferred_element_type=jnp.float32,
            )
            chosen = weight[pl.ds(off, K_INP), c : c + w]
            total[pl.ds(k, K_STEP), c : c + w] = jnp.sum(
                inner.reshape(K_STEP, K_INP, w) * chosen[None], axis=1
            )

    blocks = []
    for n, (d, own, _) in enumerate(plan):
        owner = lax.rem(z - d * (1 - 2 * core) + NZ, NZ)
        blocks.append((own, owner, pack(total[:, n * BLOCK : (n + 1) * BLOCK])))

    @pl.when(odd == core)
    def _():
        for own, owner, block in blocks:
            (keep if own else give)[owner] = block

    @pl.when(odd != core)
    def _():
        for own, owner, block in blocks:
            (give if own else keep)[owner] = block


def partial_sums(plan, where, tensor, pieces, before):
    size = BLOCK * len(plan)
    first_call = before is None
    args = [where, tensor, *pieces]
    in_specs = [SMEM] + [HBM if first_call else VMEM] * (1 + len(pieces))
    part = jax.ShapeDtypeStruct((NZ, 48, 128), jnp.float32)
    out_shape, aliases = [part, part], {}
    scratch = [
        pltpu.VMEM((size, 1024), jnp.bfloat16),
        pltpu.VMEM((128, size), jnp.float32),
        pltpu.VMEM((K_OUT, size), jnp.float32),
    ]
    if first_call:
        out_shape.append(jax.ShapeDtypeStruct(tensor.shape, tensor.dtype))
        scratch.append(pltpu.SemaphoreType.DMA((2,)))
    else:
        aliases = {len(args): 0, len(args) + 1: 1}
        args += before
        in_specs += [VMEM, VMEM]
    return pl.pallas_call(
        functools.partial(collide, plan, first_call, len(pieces)),
        in_specs=in_specs,
        out_specs=[VMEM] * len(out_shape),
        out_shape=out_shape,
        input_output_aliases=aliases,
        scratch_shapes=scratch,
        compiler_params=pltpu.CompilerParams(vmem_limit_bytes=16 << 20),
        cost_estimate=pl.CostEstimate(
            flops=2 * K_OUT * K_INP * 1024 * size,
            bytes_accessed=tensor.size * 4 if first_call else 1 << 20,
            transcendentals=0,
        ),
    )(*args)


def whole(piece, source=0):
    return ((piece, source, BLOCK, None),)


def halves(mine, theirs, source):
    return ((mine, source, HALF, 0), (theirs, source, HALF, 1))


def add_pair(mine, theirs, out):
    out[...] = mine[...] + theirs[...]


def add_up(shares, out):
    out[...] = unpack(jnp.sum(shares[...], axis=0)).astype(jnp.bfloat16)


def local(tensor, state):
    out_at, inp_at = lax.axis_index("out"), lax.axis_index("inp")
    z, odd, core = out_at // 2, out_at % 2, inp_at % 2
    start = core * HALF
    where = jnp.stack([inp_at * K_INP, z, odd, core, start]).astype(jnp.int32)

    def half(array):
        return lax.dynamic_slice(
            array, (start, 0), (HALF, array.shape[1]), allow_negative_indices=False
        )

    two = along_z(state, 2)
    one = along_z(state, 1)
    same_x = along_x(state)
    there = [pltpu.with_memory_space_constraint(a, pltpu.HBM) for a in (tensor, state)]
    give, keep, held = partial_sums(((0, True, ()),), where, there[0], there[1:], None)

    one, two, same_x, give = lax.optimization_barrier((one, two, same_x, give))
    near = rows(one, two)
    near_swap = swap(near)
    both = rows(one, half(two))
    near, both = lax.optimization_barrier((near, both))
    far = along_z(both, 2)
    near_x = along_x(near)
    plan = (
        (1, True, whole(0)),
        (2, True, whole(0, BLOCK)),
        (-1, True, whole(1)),
        (-2, True, whole(1, BLOCK)),
        (0, False, whole(2)),
    )
    give, keep = partial_sums(plan, where, held, [near, near_swap, same_x], [give, keep])

    far, give = lax.optimization_barrier((far, give))
    far_x = along_x(far)
    far_swap = swap(far)
    near_x_swap = swap(near_x)
    plan = (
        (3, True, whole(0)),
        (-3, True, whole(1)),
        (4, True, halves(0, 1, BLOCK)),
        (1, False, whole(2)),
        (2, False, whole(2, BLOCK)),
    )
    give, keep = partial_sums(plan, where, held, [far, far_swap, near_x], [give, keep])

    far_x, give = lax.optimization_barrier((far_x, give))
    far_x_swap = swap(far_x)
    plan = (
        (-1, False, whole(0)),
        (-2, False, whole(0, BLOCK)),
        (3, False, whole(1)),
        (-3, False, whole(2)),
        (4, False, halves(1, 2, BLOCK)),
    )
    give, keep = partial_sums(
        plan, where, held, [near_x_swap, far_x, far_x_swap], [give, keep]
    )

    got = swap(give)
    pair = pl.pallas_call(
        add_pair,
        in_specs=[VMEM, VMEM],
        out_specs=VMEM,
        out_shape=jax.ShapeDtypeStruct(keep.shape, keep.dtype),
        compiler_params=SMALL,
    )(keep, got)
    groups = [[c + NC * i for i in range(NZ)] for c in range(NC)]
    shares = lax.all_to_all(pair, "inp", 0, 0, tiled=True, axis_index_groups=groups)
    done = pl.pallas_call(
        add_up,
        in_specs=[VMEM],
        out_specs=VMEM,
        out_shape=jax.ShapeDtypeStruct((K_OUT, BLOCK), jnp.bfloat16),
        compiler_params=SMALL,
    )(shares)
    return done.T


def solution(mesh):
    placed = (P("out", "inp", None), P("out", None))
    return jax.shard_map(
        local, mesh=mesh, in_specs=placed, out_specs=P("inp", "out"), check_vma=False
    )
```

```python
import functools
from typing import NamedTuple

import jax
import jax.numpy as jnp
from jax import lax
from jax.experimental import pallas as pl
from jax.experimental.pallas import tpu as pltpu
from jax.sharding import PartitionSpec as P

NZ, NX, NY, NC = 8, 4, 4, 2
AXES = ("out", "inp")
BLOCK = 96
HALF = BLOCK // 2
K_OUT = 64
K_INP = 64
K_STEP = 32
TILE = 256
VMEM = pl.BlockSpec(memory_space=pltpu.VMEM)
SMEM = pl.BlockSpec(memory_space=pltpu.SMEM)
HBM = pl.BlockSpec(memory_space=pltpu.HBM)

SMALL = pltpu.CompilerParams(vmem_limit_bytes=4 << 20)


def device(x, y, z, core):
    out = (z % NZ) * 2 + (x % NX) % 2
    inp = (y % NY) * 4 + ((x % NX) // 2) * 2 + core % NC
    return out * 16 + inp


def hop(way):
    pairs = []
    for z in range(NZ):
        for y in range(NY):
            for x in range(NX):
                for c in range(NC):
                    dx, dy, dz, dc = way(c)
                    pairs.append((device(x, y, z, c), device(x + dx, y + dy, z + dz, c + dc)))
    return pairs


def sign(core):
    return 1 - 2 * core


def along_z(array, d):
    return lax.ppermute(array, AXES, hop(lambda c: (0, 0, d * sign(c), 0)))


def along_x(array):
    return lax.ppermute(array, AXES, hop(lambda c: (sign(c), 0, 0, 0)))


def swap(array):
    return lax.ppermute(array, AXES, hop(lambda c: (0, 0, 0, 1)))


def rows(*arrays):
    return jnp.concatenate(arrays, axis=0)


def pack(block):
    last = block[48:64]
    side = jnp.concatenate([last[:, 0:32], last[:, 32:64], last[:, 64:96]], axis=0)
    return jnp.concatenate([block[0:48], side], axis=1)


def unpack(packed):
    side = packed[:, 96:128]
    last = jnp.concatenate([side[0:16], side[16:32], side[32:48]], axis=1)
    return jnp.concatenate([packed[:, 0:96], last], axis=0)


def collide(call, where, *refs):
    refs = list(refs)
    tensor_in = refs.pop(0)
    n = len({part[0] for part in call.parts})
    pieces, refs = refs[:n], refs[n:]
    if call.kind == "first":
        give, keep, tensor, cells, weight, total, arrived = refs
        copies = [
            pltpu.make_async_copy(pieces[0], cells, arrived.at[0]),
            pltpu.make_async_copy(tensor_in, tensor, arrived.at[1]),
        ]
        for copy in copies:
            copy.start()
        for copy in copies:
            copy.wait()
    else:
        tensor = tensor_in
        if call.kind == "open":
            _, _, give, keep, total, cells, weight = refs
        elif call.kind == "close":
            _, _, _, give, keep, total, cells, weight = refs
        else:
            _, _, give, keep, cells, weight, total = refs
        core = where[3]
        for piece, source, count, at, half in call.parts:
            at -= call.low
            if half is not None:
                at = pl.multiple_of(at + (core if half == 0 else 1 - core) * HALF, 16)
            cells[pl.ds(at, count), :] = pieces[piece][source : source + count, :]
    first, z, odd, core = where[0], where[1], where[2], where[3]
    base = pl.multiple_of((first // 128) * 128, 128)
    weight[...] = cells[:, pl.ds(base, 128)].astype(jnp.float32).T
    off = pl.multiple_of(lax.rem(first, 128), K_INP)
    size = cells.shape[0]

    for k in range(0, K_OUT, K_STEP):
        left = tensor[pl.ds(k, K_STEP)].reshape(K_STEP * K_INP, tensor.shape[2])
        for c in range(0, size, TILE):
            w = min(TILE, size - c)
            inner = lax.dot_general(
                left,
                cells[c : c + w, :],
                (((1,), (1,)), ((), ())),
                preferred_element_type=jnp.float32,
            )
            chosen = weight[pl.ds(off, K_INP), c : c + w]
            total[pl.ds(k, K_STEP), call.low + c : call.low + c + w] = jnp.sum(
                inner.reshape(K_STEP, K_INP, w) * chosen[None], axis=1
            )

    blocks = []
    for at, d, own in call.blocks:
        owner = lax.rem(z - d * (1 - 2 * core) + NZ, NZ)
        blocks.append((own, owner, pack(total[:, at : at + BLOCK])))

    @pl.when(odd == core)
    def _():
        for own, owner, block in blocks:
            (keep if own else give)[owner] = block

    @pl.when(odd != core)
    def _():
        for own, owner, block in blocks:
            (give if own else keep)[owner] = block


class Call(NamedTuple):
    kind: str
    low: int
    high: int
    parts: tuple
    blocks: tuple


def partial_sums(call, where, tensor, pieces, before):
    size = call.high - call.low
    first_call = call.kind == "first"
    args = [where, tensor, *pieces]
    in_specs = [SMEM] + [HBM if first_call else VMEM] * (1 + len(pieces))
    part = jax.ShapeDtypeStruct((NZ, 48, 128), jnp.float32)
    out_shape = [part, part]
    scratch = [
        pltpu.VMEM((size, 1024), jnp.bfloat16),
        pltpu.VMEM((128, size), jnp.float32),
    ]
    if call.kind in ("open", "close"):
        out_shape.append(jax.ShapeDtypeStruct((K_OUT, 2 * TILE), jnp.float32))
    else:
        scratch.append(pltpu.VMEM((K_OUT, size), jnp.float32))
    if first_call:
        out_shape.append(jax.ShapeDtypeStruct(tensor.shape, tensor.dtype))
        scratch.append(pltpu.SemaphoreType.DMA((2,)))
    aliases = {len(args) + n: n for n in range(len(before))}
    args += before
    in_specs += [VMEM] * len(before)
    return pl.pallas_call(
        functools.partial(collide, call),
        in_specs=in_specs,
        out_specs=[VMEM] * len(out_shape),
        out_shape=out_shape,
        input_output_aliases=aliases,
        scratch_shapes=scratch,
        compiler_params=pltpu.CompilerParams(vmem_limit_bytes=16 << 20),
        cost_estimate=pl.CostEstimate(
            flops=2 * K_OUT * K_INP * 1024 * size,
            bytes_accessed=tensor.size * 4 if first_call else 1 << 20,
            transcendentals=0,
        ),
    )(*args)


def far_calls(near_blocks):
    at = [n * BLOCK for n in range(5)]
    early = TILE - at[2]
    first = Call(
        "open",
        0,
        TILE,
        ((0, 0, 2 * BLOCK, 0, None), (1, 0, early, at[2], None)),
        tuple((at[n], d, own) for n, (d, own) in enumerate(near_blocks[:2])),
    )
    second = Call(
        "close",
        TILE,
        5 * BLOCK,
        (
            (0, early, BLOCK - early, TILE, None),
            (1, 0, BLOCK, at[3], None),
            (0, BLOCK, HALF, at[4], 0),
            (1, BLOCK, HALF, at[4], 1),
        ),
        tuple((at[2 + n], d, near_blocks[2]) for n, d in enumerate((3, -3, 4))),
    )
    return first, second


def add_pair(mine, theirs, out):
    out[...] = mine[...] + theirs[...]


def add_up(shares, out):
    out[...] = unpack(jnp.sum(shares[...], axis=0)).astype(jnp.bfloat16)


def local(tensor, state):
    out_at, inp_at = lax.axis_index("out"), lax.axis_index("inp")
    z, odd, core = out_at // 2, out_at % 2, inp_at % 2
    start = core * HALF
    where = jnp.stack([inp_at * K_INP, z, odd, core, start]).astype(jnp.int32)

    def half(array):
        return lax.dynamic_slice(
            array, (start, 0), (HALF, array.shape[1]), allow_negative_indices=False
        )

    two = along_z(state, 2)
    one = along_z(state, 1)
    same_x = along_x(state)
    there = [pltpu.with_memory_space_constraint(a, pltpu.HBM) for a in (tensor, state)]
    give, keep, held = partial_sums(
        Call("first", 0, BLOCK, ((0, 0, BLOCK, 0, None),), ((0, 0, True),)), where, there[0], there[1:], []
    )

    one, two, same_x, give = lax.optimization_barrier((one, two, same_x, give))
    near = rows(one, two)
    near_swap = swap(near)
    both = rows(one, half(two))
    near, both = lax.optimization_barrier((near, both))
    far = along_z(both, 2)
    near_x = along_x(near)
    call = Call(
        "plain",
        0,
        5 * BLOCK,
        (
            (0, 0, 2 * BLOCK, 0, None),
            (1, 0, 2 * BLOCK, 2 * BLOCK, None),
            (2, 0, BLOCK, 4 * BLOCK, None),
        ),
        tuple(
            (n * BLOCK, d, own)
            for n, (d, own) in enumerate(
                ((1, True), (2, True), (-1, True), (-2, True), (0, False))
            )
        ),
    )
    give, keep = partial_sums(call, where, held, [near, near_swap, same_x], [give, keep])

    far, give = lax.optimization_barrier((far, give))
    far_x = along_x(far)
    far_swap = swap(far)
    near_x_swap = swap(near_x)
    call = Call(
        "plain",
        0,
        5 * BLOCK,
        (
            (0, 0, 2 * BLOCK, 0, None),
            (1, 0, BLOCK, 2 * BLOCK, None),
            (2, 0, BLOCK, 3 * BLOCK, None),
            (1, BLOCK, HALF, 4 * BLOCK, 0),
            (2, BLOCK, HALF, 4 * BLOCK, 1),
        ),
        tuple(
            (n * BLOCK, d, own)
            for n, (d, own) in enumerate(
                ((1, False), (2, False), (3, True), (-3, True), (4, True))
            )
        ),
    )
    give, keep = partial_sums(call, where, held, [near_x, far, far_swap], [give, keep])

    far_x, give = lax.optimization_barrier((far_x, give))
    far_x_swap = swap(far_x)
    first, second = far_calls(((-1, False), (-2, False), False))
    give, keep, sums = partial_sums(
        first, where, held, [near_x_swap, far_x], [give, keep]
    )
    give, keep, sums = partial_sums(
        second, where, held, [far_x, far_x_swap], [give, keep, sums]
    )

    got = swap(give)
    pair = pl.pallas_call(
        add_pair,
        in_specs=[VMEM, VMEM],
        out_specs=VMEM,
        out_shape=jax.ShapeDtypeStruct(keep.shape, keep.dtype),
        compiler_params=SMALL,
    )(keep, got)
    groups = [[c + NC * i for i in range(NZ)] for c in range(NC)]
    shares = lax.all_to_all(pair, "inp", 0, 0, tiled=True, axis_index_groups=groups)
    done = pl.pallas_call(
        add_up,
        in_specs=[VMEM],
        out_specs=VMEM,
        out_shape=jax.ShapeDtypeStruct((K_OUT, BLOCK), jnp.bfloat16),
        compiler_params=SMALL,
    )(shares)
    return done.T


def solution(mesh):
    placed = (P("out", "inp", None), P("out", None))
    return jax.shard_map(
        local, mesh=mesh, in_specs=placed, out_specs=P("inp", "out"), check_vma=False
    )
```

```python
import functools
from typing import NamedTuple

import jax
import jax.numpy as jnp
from jax import lax
from jax.experimental import pallas as pl
from jax.experimental.pallas import tpu as pltpu
from jax.sharding import PartitionSpec as P

NZ, NX, NY, NC = 8, 4, 4, 2
AXES = ("out", "inp")
BLOCK = 96
HALF = BLOCK // 2
K_OUT = 64
K_INP = 64
K_STEP = 64
TILE = 256
VMEM = pl.BlockSpec(memory_space=pltpu.VMEM)
SMEM = pl.BlockSpec(memory_space=pltpu.SMEM)
HBM = pl.BlockSpec(memory_space=pltpu.HBM)

SMALL = pltpu.CompilerParams(vmem_limit_bytes=4 << 20)


def device(x, y, z, core):
    out = (z % NZ) * 2 + (x % NX) % 2
    inp = (y % NY) * 4 + ((x % NX) // 2) * 2 + core % NC
    return out * 16 + inp


def hop(way):
    pairs = []
    for z in range(NZ):
        for y in range(NY):
            for x in range(NX):
                for c in range(NC):
                    dx, dy, dz, dc = way(c, x)
                    pairs.append((device(x, y, z, c), device(x + dx, y + dy, z + dz, c + dc)))
    return pairs


def sign(core):
    return 1 - 2 * core


def along_z(array, d):
    return lax.ppermute(array, AXES, hop(lambda c, x: (0, 0, d * sign(c), 0)))


def along_x(array):
    return lax.ppermute(array, AXES, hop(lambda c, x: (sign((x + c) % 2), 0, 0, 0)))


def swap(array):
    return lax.ppermute(array, AXES, hop(lambda c, x: (0, 0, 0, 1)))


def rows(*arrays):
    return jnp.concatenate(arrays, axis=0)


def pack(block):
    last = block[48:64]
    side = jnp.concatenate([last[:, 0:32], last[:, 32:64], last[:, 64:96]], axis=0)
    return jnp.concatenate([block[0:48], side], axis=1)


def unpack(packed):
    side = packed[:, 96:128]
    last = jnp.concatenate([side[0:16], side[16:32], side[32:48]], axis=1)
    return jnp.concatenate([packed[:, 0:96], last], axis=0)


def collide(call, where, *refs):
    refs = list(refs)
    tensor_in = refs.pop(0)
    n = len({part[0] for part in call.parts})
    pieces, refs = refs[:n], refs[n:]
    if call.kind == "first":
        give, keep, tensor, cells, weight, total, arrived = refs
        copies = [
            pltpu.make_async_copy(pieces[0], cells, arrived.at[0]),
            pltpu.make_async_copy(tensor_in, tensor, arrived.at[1]),
        ]
        for copy in copies:
            copy.start()
        for copy in copies:
            copy.wait()
    else:
        tensor = tensor_in
        if call.kind == "open":
            _, _, give, keep, total, cells, weight = refs
        elif call.kind == "close":
            _, _, _, give, keep, total, cells, weight = refs
        else:
            _, _, give, keep, cells, weight, total = refs
        core = where[3]
        for piece, source, count, at, half in call.parts:
            at -= call.low
            if half is not None:
                at = pl.multiple_of(at + (core if half == 0 else 1 - core) * HALF, 16)
            cells[pl.ds(at, count), :] = pieces[piece][source : source + count, :]
    first, z, odd, core = where[0], where[1], where[2], where[3]
    base = pl.multiple_of((first // 128) * 128, 128)
    weight[...] = cells[:, pl.ds(base, 128)].astype(jnp.float32).T
    off = pl.multiple_of(lax.rem(first, 128), K_INP)
    size = cells.shape[0]

    for k in range(0, K_OUT, K_STEP):
        left = tensor[pl.ds(k, K_STEP)].reshape(K_STEP * K_INP, tensor.shape[2])
        for c in range(0, size, TILE):
            w = min(TILE, size - c)
            inner = lax.dot_general(
                left,
                cells[c : c + w, :],
                (((1,), (1,)), ((), ())),
                preferred_element_type=jnp.float32,
            )
            chosen = weight[pl.ds(off, K_INP), c : c + w]
            total[pl.ds(k, K_STEP), call.low + c : call.low + c + w] = jnp.sum(
                inner.reshape(K_STEP, K_INP, w) * chosen[None], axis=1
            )

    blocks = []
    for at, d, own in call.blocks:
        owner = lax.rem(z - d * (1 - 2 * core) + NZ, NZ)
        blocks.append((own, owner, pack(total[:, at : at + BLOCK])))

    @pl.when(odd == core)
    def _():
        for own, owner, block in blocks:
            (keep if own else give)[owner] = block

    @pl.when(odd != core)
    def _():
        for own, owner, block in blocks:
            (give if own else keep)[owner] = block


class Call(NamedTuple):
    kind: str
    low: int
    high: int
    parts: tuple
    blocks: tuple


def partial_sums(call, where, tensor, pieces, before):
    size = call.high - call.low
    first_call = call.kind == "first"
    args = [where, tensor, *pieces]
    in_specs = [SMEM] + [HBM if first_call else VMEM] * (1 + len(pieces))
    part = jax.ShapeDtypeStruct((NZ, 48, 128), jnp.float32)
    out_shape = [part, part]
    scratch = [
        pltpu.VMEM((size, 1024), jnp.bfloat16),
        pltpu.VMEM((128, size), jnp.float32),
    ]
    if call.kind in ("open", "close"):
        out_shape.append(jax.ShapeDtypeStruct((K_OUT, 2 * TILE), jnp.float32))
    else:
        scratch.append(pltpu.VMEM((K_OUT, size), jnp.float32))
    if first_call:
        out_shape.append(jax.ShapeDtypeStruct(tensor.shape, tensor.dtype))
        scratch.append(pltpu.SemaphoreType.DMA((2,)))
    aliases = {len(args) + n: n for n in range(len(before))}
    args += before
    in_specs += [VMEM] * len(before)
    return pl.pallas_call(
        functools.partial(collide, call),
        in_specs=in_specs,
        out_specs=[VMEM] * len(out_shape),
        out_shape=out_shape,
        input_output_aliases=aliases,
        scratch_shapes=scratch,
        compiler_params=pltpu.CompilerParams(vmem_limit_bytes=16 << 20),
        cost_estimate=pl.CostEstimate(
            flops=2 * K_OUT * K_INP * 1024 * size,
            bytes_accessed=tensor.size * 4 if first_call else 1 << 20,
            transcendentals=0,
        ),
    )(*args)


def far_calls(near_blocks):
    at = [n * BLOCK for n in range(5)]
    early = TILE - at[2]
    first = Call(
        "open",
        0,
        TILE,
        ((0, 0, 2 * BLOCK, 0, None), (1, 0, early, at[2], None)),
        tuple((at[n], d, own) for n, (d, own) in enumerate(near_blocks[:2])),
    )
    second = Call(
        "close",
        TILE,
        5 * BLOCK,
        (
            (0, early, BLOCK - early, TILE, None),
            (1, 0, BLOCK, at[3], None),
            (0, BLOCK, HALF, at[4], 0),
            (1, BLOCK, HALF, at[4], 1),
        ),
        tuple((at[2 + n], d, near_blocks[2]) for n, d in enumerate((3, -3, 4))),
    )
    return first, second


def add_pair(mine, theirs, out):
    out[...] = mine[...] + theirs[...]


def local(tensor, state):
    out_at, inp_at = lax.axis_index("out"), lax.axis_index("inp")
    z, odd, core = out_at // 2, out_at % 2, inp_at % 2
    start = core * HALF
    where = jnp.stack([inp_at * K_INP, z, odd, core, start]).astype(jnp.int32)

    def half(array):
        return lax.dynamic_slice(
            array, (start, 0), (HALF, array.shape[1]), allow_negative_indices=False
        )

    two = along_z(state, 2)
    one = along_z(state, 1)
    same_x = along_x(state)
    there = [pltpu.with_memory_space_constraint(a, pltpu.HBM) for a in (tensor, state)]
    give, keep, held = partial_sums(
        Call("first", 0, BLOCK, ((0, 0, BLOCK, 0, None),), ((0, 0, True),)), where, there[0], there[1:], []
    )

    one, two, same_x, give = lax.optimization_barrier((one, two, same_x, give))
    near = rows(one, two)
    near_swap = swap(near)
    both = rows(one, half(two))
    near, both = lax.optimization_barrier((near, both))
    far = along_z(both, 2)
    near_x = along_x(near)
    call = Call(
        "plain",
        0,
        5 * BLOCK,
        (
            (0, 0, 2 * BLOCK, 0, None),
            (1, 0, 2 * BLOCK, 2 * BLOCK, None),
            (2, 0, BLOCK, 4 * BLOCK, None),
        ),
        tuple(
            (n * BLOCK, d, own)
            for n, (d, own) in enumerate(
                ((1, True), (2, True), (-1, True), (-2, True), (0, False))
            )
        ),
    )
    give, keep = partial_sums(call, where, held, [near, near_swap, same_x], [give, keep])

    far, give = lax.optimization_barrier((far, give))
    far_x = along_x(far)
    far_swap = swap(far)
    near_x_swap = swap(near_x)
    call = Call(
        "plain",
        0,
        5 * BLOCK,
        (
            (0, 0, 2 * BLOCK, 0, None),
            (1, 0, BLOCK, 2 * BLOCK, None),
            (2, 0, BLOCK, 3 * BLOCK, None),
            (1, BLOCK, HALF, 4 * BLOCK, 0),
            (2, BLOCK, HALF, 4 * BLOCK, 1),
        ),
        tuple(
            (n * BLOCK, d, own)
            for n, (d, own) in enumerate(
                ((1, False), (2, False), (3, True), (-3, True), (4, True))
            )
        ),
    )
    give, keep = partial_sums(call, where, held, [near_x, far, far_swap], [give, keep])

    far_x, give = lax.optimization_barrier((far_x, give))
    far_x_swap = swap(far_x)
    first, second = far_calls(((-1, False), (-2, False), False))
    give, keep, sums = partial_sums(
        first, where, held, [near_x_swap, far_x], [give, keep]
    )
    give, keep, sums = partial_sums(
        second, where, held, [far_x, far_x_swap], [give, keep, sums]
    )

    got = swap(give)
    pair = pl.pallas_call(
        add_pair,
        in_specs=[VMEM, VMEM],
        out_specs=VMEM,
        out_shape=jax.ShapeDtypeStruct(keep.shape, keep.dtype),
        compiler_params=SMALL,
    )(keep, got)
    groups = [[c + NC * i for i in range(NZ)] for c in range(NC)]
    shares = lax.all_to_all(pair, "inp", 0, 0, tiled=True, axis_index_groups=groups)
    done = unpack(jnp.sum(shares, axis=0)).astype(jnp.bfloat16)
    return done.T


def solution(mesh):
    placed = (P("out", "inp", None), P("out", None))
    return jax.shard_map(
        local, mesh=mesh, in_specs=placed, out_specs=P("inp", "out"), check_vma=False
    )
```

```python
import functools
from typing import NamedTuple

import jax
import jax.numpy as jnp
from jax import lax
from jax.experimental import pallas as pl
from jax.experimental.pallas import tpu as pltpu
from jax.sharding import PartitionSpec as P

NZ, NX, NY, NC = 8, 4, 4, 2
AXES = ("out", "inp")
BLOCK = 96
HALF = BLOCK // 2
K_OUT = 64
K_INP = 64
K_STEP = 64
TILE = 256
VMEM = pl.BlockSpec(memory_space=pltpu.VMEM)
SMEM = pl.BlockSpec(memory_space=pltpu.SMEM)
HBM = pl.BlockSpec(memory_space=pltpu.HBM)

SMALL = pltpu.CompilerParams(vmem_limit_bytes=4 << 20)


def device(x, y, z, core):
    out = (z % NZ) * 2 + (x % NX) % 2
    inp = (y % NY) * 4 + ((x % NX) // 2) * 2 + core % NC
    return out * 16 + inp


def hop(way):
    pairs = []
    for z in range(NZ):
        for y in range(NY):
            for x in range(NX):
                for c in range(NC):
                    dx, dy, dz, dc = way(c, x)
                    pairs.append((device(x, y, z, c), device(x + dx, y + dy, z + dz, c + dc)))
    return pairs


def sign(core):
    return 1 - 2 * core


def along_z(array, d):
    return lax.ppermute(array, AXES, hop(lambda c, x: (0, 0, d * sign(c), 0)))


def along_x(array):
    return lax.ppermute(array, AXES, hop(lambda c, x: (sign((x + c) % 2), 0, 0, 0)))


def swap(array):
    return lax.ppermute(array, AXES, hop(lambda c, x: (0, 0, 0, 1)))


def rows(*arrays):
    return jnp.concatenate(arrays, axis=0)


def pack(block):
    last = block[48:64]
    side = jnp.concatenate([last[:, 0:32], last[:, 32:64], last[:, 64:96]], axis=0)
    return jnp.concatenate([block[0:48], side], axis=1)


def unpack(packed):
    side = packed[:, 96:128]
    last = jnp.concatenate([side[0:16], side[16:32], side[32:48]], axis=1)
    return jnp.concatenate([packed[:, 0:96], last], axis=0)


def collide(call, where, *refs):
    refs = list(refs)
    tensor_in = refs.pop(0)
    n = len({part[0] for part in call.parts})
    pieces, refs = refs[:n], refs[n:]
    if call.kind == "first":
        give, keep, tensor, cells, weight, total, arrived = refs
        copies = [
            pltpu.make_async_copy(pieces[0], cells, arrived.at[0]),
            pltpu.make_async_copy(tensor_in, tensor, arrived.at[1]),
        ]
        for copy in copies:
            copy.start()
        for copy in copies:
            copy.wait()
    else:
        tensor = tensor_in
        if call.kind == "open":
            _, _, give, keep, total, cells, weight = refs
        elif call.kind == "close":
            _, _, _, give, keep, total, cells, weight = refs
        else:
            _, _, give, keep, cells, weight, total = refs
        core = where[3]
        for piece, source, count, at, half in call.parts:
            at -= call.low
            if half is not None:
                at = pl.multiple_of(at + (core if half == 0 else 1 - core) * HALF, 16)
            cells[pl.ds(at, count), :] = pieces[piece][source : source + count, :]
    first, z, odd, core = where[0], where[1], where[2], where[3]
    base = pl.multiple_of((first // 128) * 128, 128)
    weight[...] = cells[:, pl.ds(base, 128)].astype(jnp.float32).T
    off = pl.multiple_of(lax.rem(first, 128), K_INP)
    size = cells.shape[0]

    for k in range(0, K_OUT, K_STEP):
        left = tensor[pl.ds(k, K_STEP)].reshape(K_STEP * K_INP, tensor.shape[2])
        for c in range(0, size, TILE):
            w = min(TILE, size - c)
            inner = lax.dot_general(
                left,
                cells[c : c + w, :],
                (((1,), (1,)), ((), ())),
                preferred_element_type=jnp.float32,
            )
            chosen = weight[pl.ds(off, K_INP), c : c + w]
            total[pl.ds(k, K_STEP), call.low + c : call.low + c + w] = jnp.sum(
                inner.reshape(K_STEP, K_INP, w) * chosen[None], axis=1
            )

    blocks = []
    for at, d, own in call.blocks:
        owner = lax.rem(z - d * (1 - 2 * core) + NZ, NZ)
        blocks.append((own, owner, pack(total[:, at : at + BLOCK])))

    @pl.when(odd == core)
    def _():
        for own, owner, block in blocks:
            (keep if own else give)[owner] = block

    @pl.when(odd != core)
    def _():
        for own, owner, block in blocks:
            (give if own else keep)[owner] = block


class Call(NamedTuple):
    kind: str
    low: int
    high: int
    parts: tuple
    blocks: tuple


def partial_sums(call, where, tensor, pieces, before):
    size = call.high - call.low
    first_call = call.kind == "first"
    args = [where, tensor, *pieces]
    in_specs = [SMEM] + [HBM if first_call else VMEM] * (1 + len(pieces))
    part = jax.ShapeDtypeStruct((NZ, 48, 128), jnp.float32)
    out_shape = [part, part]
    scratch = [
        pltpu.VMEM((size, 1024), jnp.bfloat16),
        pltpu.VMEM((128, size), jnp.float32),
    ]
    if call.kind in ("open", "close"):
        out_shape.append(jax.ShapeDtypeStruct((K_OUT, 2 * TILE), jnp.float32))
    else:
        scratch.append(pltpu.VMEM((K_OUT, size), jnp.float32))
    if first_call:
        out_shape.append(jax.ShapeDtypeStruct(tensor.shape, tensor.dtype))
        scratch.append(pltpu.SemaphoreType.DMA((2,)))
    aliases = {len(args) + n: n for n in range(len(before))}
    args += before
    in_specs += [VMEM] * len(before)
    return pl.pallas_call(
        functools.partial(collide, call),
        in_specs=in_specs,
        out_specs=[VMEM] * len(out_shape),
        out_shape=out_shape,
        input_output_aliases=aliases,
        scratch_shapes=scratch,
        compiler_params=pltpu.CompilerParams(vmem_limit_bytes=16 << 20),
        cost_estimate=pl.CostEstimate(
            flops=2 * K_OUT * K_INP * 1024 * size,
            bytes_accessed=tensor.size * 4 if first_call else 1 << 20,
            transcendentals=0,
        ),
    )(*args)


def far_calls(near_blocks):
    at = [n * BLOCK for n in range(5)]
    early = TILE - at[2]
    first = Call(
        "open",
        0,
        TILE,
        ((0, 0, 2 * BLOCK, 0, None), (1, 0, early, at[2], None)),
        tuple((at[n], d, own) for n, (d, own) in enumerate(near_blocks[:2])),
    )
    second = Call(
        "close",
        TILE,
        5 * BLOCK,
        (
            (0, early, BLOCK - early, TILE, None),
            (1, 0, BLOCK, at[3], None),
            (0, BLOCK, HALF, at[4], 0),
            (1, BLOCK, HALF, at[4], 1),
        ),
        tuple((at[2 + n], d, near_blocks[2]) for n, d in enumerate((3, -3, 4))),
    )
    return first, second


def add_pair(mine, theirs, out):
    out[...] = mine[...] + theirs[...]


def local(tensor, state):
    out_at, inp_at = lax.axis_index("out"), lax.axis_index("inp")
    z, odd, core = out_at // 2, out_at % 2, inp_at % 2
    start = core * HALF
    where = jnp.stack([inp_at * K_INP, z, odd, core, start]).astype(jnp.int32)

    def half(array):
        return lax.dynamic_slice(
            array, (start, 0), (HALF, array.shape[1]), allow_negative_indices=False
        )

    two = along_z(state, 2)
    one = along_z(state, 1)
    same_x = along_x(state)
    there = [pltpu.with_memory_space_constraint(a, pltpu.HBM) for a in (tensor, state)]
    give, keep, held = partial_sums(
        Call("first", 0, BLOCK, ((0, 0, BLOCK, 0, None),), ((0, 0, True),)), where, there[0], there[1:], []
    )

    one, two, same_x, give = lax.optimization_barrier((one, two, same_x, give))
    near = rows(one, two)
    hops = half(two)
    near, two, hops = lax.optimization_barrier((near, two, hops))
    four = along_z(hops, 2)
    three = along_z(two, 1)
    near_x = along_x(near)
    near_swap = swap(near)
    call = Call(
        "plain",
        0,
        5 * BLOCK,
        (
            (0, 0, 2 * BLOCK, 0, None),
            (1, 0, 2 * BLOCK, 2 * BLOCK, None),
            (2, 0, BLOCK, 4 * BLOCK, None),
        ),
        tuple(
            (n * BLOCK, d, own)
            for n, (d, own) in enumerate(
                ((1, True), (2, True), (-1, True), (-2, True), (0, False))
            )
        ),
    )
    give, keep = partial_sums(call, where, held, [near, near_swap, same_x], [give, keep])

    three, four, give = lax.optimization_barrier((three, four, give))
    far = rows(three, four)
    far_x = along_x(far)
    far_swap = swap(far)
    near_x_swap = swap(near_x)
    call = Call(
        "plain",
        0,
        5 * BLOCK,
        (
            (0, 0, 2 * BLOCK, 0, None),
            (1, 0, BLOCK, 2 * BLOCK, None),
            (2, 0, BLOCK, 3 * BLOCK, None),
            (1, BLOCK, HALF, 4 * BLOCK, 0),
            (2, BLOCK, HALF, 4 * BLOCK, 1),
        ),
        tuple(
            (n * BLOCK, d, own)
            for n, (d, own) in enumerate(
                ((1, False), (2, False), (3, True), (-3, True), (4, True))
            )
        ),
    )
    give, keep = partial_sums(call, where, held, [near_x, far, far_swap], [give, keep])

    far_x, give = lax.optimization_barrier((far_x, give))
    far_x_swap = swap(far_x)
    first, second = far_calls(((-1, False), (-2, False), False))
    give, keep, sums = partial_sums(
        first, where, held, [near_x_swap, far_x], [give, keep]
    )
    give, keep, sums = partial_sums(
        second, where, held, [far_x, far_x_swap], [give, keep, sums]
    )

    got = swap(give)
    pair = pl.pallas_call(
        add_pair,
        in_specs=[VMEM, VMEM],
        out_specs=VMEM,
        out_shape=jax.ShapeDtypeStruct(keep.shape, keep.dtype),
        compiler_params=SMALL,
    )(keep, got)
    groups = [[c + NC * i for i in range(NZ)] for c in range(NC)]
    shares = lax.all_to_all(pair, "inp", 0, 0, tiled=True, axis_index_groups=groups)
    done = unpack(jnp.sum(shares, axis=0)).astype(jnp.bfloat16)
    return done.T


def solution(mesh):
    placed = (P("out", "inp", None), P("out", None))
    return jax.shard_map(
        local, mesh=mesh, in_specs=placed, out_specs=P("inp", "out"), check_vma=False
    )
```

```python
import functools
from typing import NamedTuple

import jax
import jax.numpy as jnp
from jax import lax
from jax.experimental import pallas as pl
from jax.experimental.pallas import tpu as pltpu
from jax.sharding import PartitionSpec as P

NZ, NX, NY, NC = 8, 4, 4, 2
AXES = ("out", "inp")
BLOCK = 96
HALF = BLOCK // 2
K_OUT = 64
K_INP = 64
K_STEP = 64
TILE = 256
VMEM = pl.BlockSpec(memory_space=pltpu.VMEM)
SMEM = pl.BlockSpec(memory_space=pltpu.SMEM)
HBM = pl.BlockSpec(memory_space=pltpu.HBM)

SMALL = pltpu.CompilerParams(vmem_limit_bytes=4 << 20)


def device(x, y, z, core):
    out = (z % NZ) * 2 + (x % NX) % 2
    inp = (y % NY) * 4 + ((x % NX) // 2) * 2 + core % NC
    return out * 16 + inp


def hop(way):
    pairs = []
    for z in range(NZ):
        for y in range(NY):
            for x in range(NX):
                for c in range(NC):
                    dx, dy, dz, dc = way(c, x)
                    pairs.append((device(x, y, z, c), device(x + dx, y + dy, z + dz, c + dc)))
    return pairs


def sign(core):
    return 1 - 2 * core


def along_z(array, d):
    return lax.ppermute(array, AXES, hop(lambda c, x: (0, 0, d * sign(c), 0)))


def along_x(array):
    return lax.ppermute(array, AXES, hop(lambda c, x: (sign((x + c) % 2), 0, 0, 0)))


def swap(array):
    return lax.ppermute(array, AXES, hop(lambda c, x: (0, 0, 0, 1)))


def rows(*arrays):
    return jnp.concatenate(arrays, axis=0)


def pack(block):
    last = block[48:64]
    side = jnp.concatenate([last[:, 0:32], last[:, 32:64], last[:, 64:96]], axis=0)
    return jnp.concatenate([block[0:48], side], axis=1)


def unpack(packed):
    side = packed[:, 96:128]
    last = jnp.concatenate([side[0:16], side[16:32], side[32:48]], axis=1)
    return jnp.concatenate([packed[:, 0:96], last], axis=0)


def collide(call, where, *refs):
    refs = list(refs)
    tensor_in = refs.pop(0)
    n = len({part[0] for part in call.parts})
    pieces, refs = refs[:n], refs[n:]
    if call.kind == "first":
        give, keep, tensor, cells, weight, total, arrived = refs
        copies = [
            pltpu.make_async_copy(pieces[0], cells, arrived.at[0]),
            pltpu.make_async_copy(tensor_in, tensor, arrived.at[1]),
        ]
        for copy in copies:
            copy.start()
        for copy in copies:
            copy.wait()
    else:
        tensor = tensor_in
        if call.kind == "open":
            _, _, give, keep, total, cells, weight = refs
        elif call.kind == "close":
            _, _, _, give, keep, total, cells, weight = refs
        else:
            _, _, give, keep, cells, weight, total = refs
        core = where[3]
        for piece, source, count, at, half in call.parts:
            at -= call.low
            if half is not None:
                at = pl.multiple_of(at + (core if half == 0 else 1 - core) * HALF, 16)
            cells[pl.ds(at, count), :] = pieces[piece][source : source + count, :]
    first, z, odd, core = where[0], where[1], where[2], where[3]
    base = pl.multiple_of((first // 128) * 128, 128)
    weight[...] = cells[:, pl.ds(base, 128)].astype(jnp.float32).T
    off = pl.multiple_of(lax.rem(first, 128), K_INP)
    size = cells.shape[0]

    for k in range(0, K_OUT, K_STEP):
        left = tensor[pl.ds(k, K_STEP)].reshape(K_STEP * K_INP, tensor.shape[2])
        for c in range(0, size, TILE):
            w = min(TILE, size - c)
            inner = lax.dot_general(
                left,
                cells[c : c + w, :],
                (((1,), (1,)), ((), ())),
                preferred_element_type=jnp.float32,
            )
            chosen = weight[pl.ds(off, K_INP), c : c + w]
            total[pl.ds(k, K_STEP), call.low + c : call.low + c + w] = jnp.sum(
                inner.reshape(K_STEP, K_INP, w) * chosen[None], axis=1
            )

    blocks = []
    for at, d, own in call.blocks:
        owner = lax.rem(z - d * (1 - 2 * core) + NZ, NZ)
        blocks.append((own, owner, pack(total[:, at : at + BLOCK])))

    @pl.when(odd == core)
    def _():
        for own, owner, block in blocks:
            (keep if own else give)[owner] = block

    @pl.when(odd != core)
    def _():
        for own, owner, block in blocks:
            (give if own else keep)[owner] = block


class Call(NamedTuple):
    kind: str
    low: int
    high: int
    parts: tuple
    blocks: tuple


def partial_sums(call, where, tensor, pieces, before):
    size = call.high - call.low
    first_call = call.kind == "first"
    args = [where, tensor, *pieces]
    in_specs = [SMEM] + [HBM if first_call else VMEM] * (1 + len(pieces))
    part = jax.ShapeDtypeStruct((NZ, 48, 128), jnp.float32)
    out_shape = [part, part]
    scratch = [
        pltpu.VMEM((size, 1024), jnp.bfloat16),
        pltpu.VMEM((128, size), jnp.float32),
    ]
    if call.kind in ("open", "close"):
        out_shape.append(jax.ShapeDtypeStruct((K_OUT, 2 * TILE), jnp.float32))
    else:
        scratch.append(pltpu.VMEM((K_OUT, size), jnp.float32))
    if first_call:
        out_shape.append(jax.ShapeDtypeStruct(tensor.shape, tensor.dtype))
        scratch.append(pltpu.SemaphoreType.DMA((2,)))
    aliases = {len(args) + n: n for n in range(len(before))}
    args += before
    in_specs += [VMEM] * len(before)
    return pl.pallas_call(
        functools.partial(collide, call),
        in_specs=in_specs,
        out_specs=[VMEM] * len(out_shape),
        out_shape=out_shape,
        input_output_aliases=aliases,
        scratch_shapes=scratch,
        compiler_params=pltpu.CompilerParams(vmem_limit_bytes=16 << 20),
        cost_estimate=pl.CostEstimate(
            flops=2 * K_OUT * K_INP * 1024 * size,
            bytes_accessed=tensor.size * 4 if first_call else 1 << 20,
            transcendentals=0,
        ),
    )(*args)


def far_calls(near_blocks):
    at = [n * BLOCK for n in range(5)]
    early = TILE - at[2]
    first = Call(
        "open",
        0,
        TILE,
        ((0, 0, 2 * BLOCK, 0, None), (1, 0, early, at[2], None)),
        tuple((at[n], d, own) for n, (d, own) in enumerate(near_blocks[:2])),
    )
    second = Call(
        "close",
        TILE,
        5 * BLOCK,
        (
            (0, early, BLOCK - early, TILE, None),
            (1, 0, BLOCK, at[3], None),
            (0, BLOCK, HALF, at[4], 0),
            (1, BLOCK, HALF, at[4], 1),
        ),
        tuple((at[2 + n], d, near_blocks[2]) for n, d in enumerate((3, -3, 4))),
    )
    return first, second


def add_pair(mine, theirs, out):
    out[...] = mine[...] + theirs[...]


def local(tensor, state):
    out_at, inp_at = lax.axis_index("out"), lax.axis_index("inp")
    z, odd, core = out_at // 2, out_at % 2, inp_at % 2
    start = core * HALF
    where = jnp.stack([inp_at * K_INP, z, odd, core, start]).astype(jnp.int32)

    def half(array):
        return lax.dynamic_slice(
            array, (start, 0), (HALF, array.shape[1]), allow_negative_indices=False
        )

    two = along_z(state, 2)
    one = along_z(state, 1)
    same_x = along_x(state)
    there = [pltpu.with_memory_space_constraint(a, pltpu.HBM) for a in (tensor, state)]
    give, keep, held = partial_sums(
        Call("first", 0, BLOCK, ((0, 0, BLOCK, 0, None),), ((0, 0, True),)), where, there[0], there[1:], []
    )

    one, two, same_x, give = lax.optimization_barrier((one, two, same_x, give))
    near = rows(one, two)
    three = along_z(two, 1)
    four = along_z(half(two), 2)
    near_swap = swap(near)
    near_x = along_x(near)
    call = Call(
        "plain",
        0,
        5 * BLOCK,
        (
            (0, 0, 2 * BLOCK, 0, None),
            (1, 0, 2 * BLOCK, 2 * BLOCK, None),
            (2, 0, BLOCK, 4 * BLOCK, None),
        ),
        tuple(
            (n * BLOCK, d, own)
            for n, (d, own) in enumerate(
                ((1, True), (2, True), (-1, True), (-2, True), (0, False))
            )
        ),
    )
    give, keep = partial_sums(call, where, held, [near, near_swap, same_x], [give, keep])

    three, four, give = lax.optimization_barrier((three, four, give))
    far = rows(three, four)
    far_x = along_x(far)
    far_swap = swap(far)
    near_x_swap = swap(near_x)
    call = Call(
        "plain",
        0,
        5 * BLOCK,
        (
            (0, 0, 2 * BLOCK, 0, None),
            (1, 0, BLOCK, 2 * BLOCK, None),
            (2, 0, BLOCK, 3 * BLOCK, None),
            (1, BLOCK, HALF, 4 * BLOCK, 0),
            (2, BLOCK, HALF, 4 * BLOCK, 1),
        ),
        tuple(
            (n * BLOCK, d, own)
            for n, (d, own) in enumerate(
                ((1, False), (2, False), (3, True), (-3, True), (4, True))
            )
        ),
    )
    give, keep = partial_sums(call, where, held, [near_x, far, far_swap], [give, keep])

    far_x, give = lax.optimization_barrier((far_x, give))
    far_x_swap = swap(far_x)
    first, second = far_calls(((-1, False), (-2, False), False))
    give, keep, sums = partial_sums(
        first, where, held, [near_x_swap, far_x], [give, keep]
    )
    give, keep, sums = partial_sums(
        second, where, held, [far_x, far_x_swap], [give, keep, sums]
    )

    got = swap(give)
    pair = pl.pallas_call(
        add_pair,
        in_specs=[VMEM, VMEM],
        out_specs=VMEM,
        out_shape=jax.ShapeDtypeStruct(keep.shape, keep.dtype),
        compiler_params=SMALL,
    )(keep, got)
    groups = [[c + NC * i for i in range(NZ)] for c in range(NC)]
    shares = lax.all_to_all(pair, "inp", 0, 0, tiled=True, axis_index_groups=groups)
    done = unpack(jnp.sum(shares, axis=0)).astype(jnp.bfloat16)
    return done.T


def solution(mesh):
    placed = (P("out", "inp", None), P("out", None))
    return jax.shard_map(
        local, mesh=mesh, in_specs=placed, out_specs=P("inp", "out"), check_vma=False
    )
```
